512 devices in a mesh: blk: 16 (over x_hi, z), grp: 32 (over y, x_lo, core).
Axes of the slice: x: 4 (x_hi: 2, x_lo: 2; x = x_hi * 2 + x_lo), y: 8, z: 8, core: 2. Of those that a mesh axis runs over, the one named last changes fastest.
Arguments:
- position: float32 [3, 262144], P(None, ('blk', 'grp')), may hold values from -6 to 6
- velocity: float32 [3, 262144], P(None, ('blk', 'grp')), may hold values from -6 to 6
- accel_old: float32 [3, 262144], P(None, ('blk', 'grp')), may hold values from -6 to 6
- jerk_old: float32 [3, 262144], P(None, ('blk', 'grp')), may hold values from -6 to 6
- mass: float32 [262144], P(('blk', 'grp')), may hold values from 1e-07 to 1e-05
- elapsed: float32 [262144], P(('blk', 'grp')), may hold values from 0.1 to 1
- active_index: int32 [8192], P(('blk', 'grp')), may hold values from 0 to 262143, as said below
Outputs:
- predicted: float32 [6, 262144], P(None, ('blk', 'grp'))
- accel: float32 [3, 8192], P(None, ('blk', 'grp'))
- jerk: float32 [3, 8192], P(None, ('blk', 'grp'))
The draws below stay inside these ranges and needn't reach their ends.
Inputs may be any that keep to these rules, and one draw needn't show every extreme that they name: `active_index`: entries 16 * k to 16 * k + 15 are distinct stars of the range 512 * k to 512 * k + 511, for every k.
All inputs are finite; a program needn't handle non-finite values.
Results may differ from the reference program's by a relative error of at most 0.0003.
Values sent between devices are 32-bit elements; how exact they have to be, the bound alone decides.
No kernel may reach another device: no remote copies, remote signals or barrier semaphores. Data moves between devices by JAX's collectives and lax.ppermute only.
A program may use at most 64 MiB of HBM per device.

```python
import math
import jax
import jax.numpy as jnp
from jax import lax

STAR_DEV = 512
ACT_DEV = 16
N_STARS = 262144


def draw_active_index(key, part):
    shards = N_STARS // STAR_DEV
    subkeys = jax.random.split(key, shards)
    picked = jax.vmap(lambda single: jax.random.permutation(single, STAR_DEV)[:ACT_DEV])(subkeys)
    offset = jnp.arange(shards, dtype=jnp.int32)[:, None] * STAR_DEV
    return (picked.astype(jnp.int32) + offset).reshape(-1)


def block_scale(stream_key, extent, cuts, low, high):
    level, own = 1.0, jax.random.fold_in(stream_key, 6)
    for axis_at, blocks in cuts:
        heights = jnp.exp(jax.random.uniform(jax.random.fold_in(own, axis_at), (blocks,), jnp.float32, low / len(cuts), high / len(cuts)))
        level = level * jnp.repeat(heights, extent[axis_at] // blocks).reshape([-1 if axis == axis_at else 1 for axis in range(len(extent))])
    return level


def gaussian(key, shape, scale, bound, cuts=(), kind=jnp.bfloat16):
    loudness = block_scale(key, shape, cuts, -0.22, 0.18) if cuts else 1.0
    drawn = jax.random.normal(key, shape, jnp.float32) * scale * loudness
    return jnp.minimum(jnp.maximum(drawn, -bound), bound).astype(kind)


def setup_inputs(seed: int = 0) -> dict:
    splits = jax.random.split(jax.random.key(seed), 8)
    position = gaussian(splits[0], (3, N_STARS), 1.0, 6.0, ((1, 512),), jnp.float32)
    velocity = gaussian(splits[1], (3, N_STARS), 0.7, 6.0, ((1, 512),), jnp.float32)
    accel_old = gaussian(splits[2], (3, N_STARS), 1.0, 6.0, ((1, 512),), jnp.float32)
    jerk_old = gaussian(splits[3], (3, N_STARS), 1.0, 6.0, ((1, 512),), jnp.float32)
    mass = jnp.clip(jnp.exp(math.log(9.999999747378752e-06) - 4.6051701 * jax.random.uniform(splits[4], (N_STARS,), jnp.float32) ** block_scale(splits[4], (N_STARS,), ((0, 512),), -0.2, 0.2)), 1.0000000116860974e-07, 9.999999747378752e-06)
    elapsed = jnp.clip(jnp.exp(math.log(1.0) - 2.3025851 * jax.random.uniform(splits[5], (N_STARS,), jnp.float32) ** block_scale(splits[5], (N_STARS,), ((0, 512),), -0.2, 0.2)), 0.1, 1.0)
    active_index = draw_active_index(jax.random.fold_in(splits[7], 71), 0)
    return dict(position=position, velocity=velocity, accel_old=accel_old, jerk_old=jerk_old, mass=mass, elapsed=elapsed, active_index=active_index)


SOFTENING = 0.0001

def predict(position, velocity, accel_old, jerk_old, elapsed):
    step_row = elapsed[None, :]
    half = step_row * step_row * 0.5
    sixth = half * step_row * (1.0 / 3.0)
    new_position = position + step_row * velocity + half * accel_old + sixth * jerk_old
    new_velocity = velocity + step_row * accel_old + half * jerk_old
    return jnp.concatenate([new_position, new_velocity], 0)

def interact(targets, sources, masses, block_limit):
    columns = targets.shape[1]
    block_size = math.gcd(columns, block_limit)
    blocks = columns // block_size
    stacked = targets.reshape(6, blocks, block_size).transpose(1, 0, 2)

    def one_block(target_block):
        separation = sources[0:3][:, None, :] - target_block[0:3][:, :, None]
        relative = sources[3:6][:, None, :] - target_block[3:6][:, :, None]
        distance = lax.optimization_barrier(jnp.sum(separation * separation, 0)) + SOFTENING
        inverse = 1.0 / jnp.sqrt(distance)
        weight = masses[None, :] * inverse * inverse * inverse
        radial = 3.0 * lax.optimization_barrier(jnp.sum(separation * relative, 0)) / distance
        accel_part = lax.optimization_barrier(jnp.sum(weight[None] * separation, 2))
        jerk_part = lax.optimization_barrier(jnp.sum(weight[None] * (relative - radial[None] * separation), 2))
        return jnp.concatenate([accel_part, jerk_part], 0)
    result = lax.map(one_block, stacked)
    return result.transpose(1, 0, 2).reshape(6, columns)

def reference(position, velocity, accel_old, jerk_old, mass, elapsed, active_index):
    predicted = predict(position, velocity, accel_old, jerk_old, elapsed)
    targets = jnp.take(predicted, active_index, axis=1)
    shards = N_STARS // STAR_DEV
    source_blocks = predicted.reshape(6, shards, STAR_DEV).transpose(1, 0, 2)
    mass_blocks = mass.reshape(shards, STAR_DEV)

    def accumulate(total, pieces):
        return (total + interact(targets, pieces[0], pieces[1], 1024), None)
    start = jnp.zeros((6, targets.shape[1]), jnp.float32)
    totals, unused = lax.scan(accumulate, start, (source_blocks, mass_blocks))
    return (predicted, totals[0:3], totals[3:6])
```

```python
import jax
import jax.numpy as jnp
from jax import lax
from jax.experimental import pallas as pl
from jax.experimental.pallas import tpu as pltpu
from jax.sharding import PartitionSpec as P

SOFTENING = 0.0001


def prologue_kernel(offsets, position, velocity, accel_old, jerk_old, mass, elapsed, predicted, sources, targets):
    step_row = elapsed[...]
    half = step_row * step_row * 0.5
    sixth = half * step_row * (1.0 / 3.0)
    new_position = position[...] + step_row * velocity[...] + half * accel_old[...] + sixth * jerk_old[...]
    new_velocity = velocity[...] + step_row * accel_old[...] + half * jerk_old[...]
    predicted[0:3, :] = new_position
    predicted[3:6, :] = new_velocity
    everything = jnp.concatenate([new_position, new_velocity, mass[...], mass[...]], 0)
    for copy in range(sources.shape[0]):
        sources[copy] = everything
    active, stars = targets.shape[1], position.shape[1]
    columns = lax.broadcasted_iota(jnp.int32, (active, stars), 1)
    chosen = columns == offsets[...]
    picked = []
    for row in range(6):
        values = jnp.broadcast_to(everything[row : row + 1], (active, stars))
        picked.append(jnp.sum(jnp.where(chosen, values, 0.0), 1, keepdims=True))
    stacked = jnp.concatenate(picked + picked[:2], 1)
    for copy in range(targets.shape[0]):
        targets[copy] = stacked


def interact_kernel(sources, targets, result):
    count, stars = sources.shape[1], sources.shape[2]
    rows = 8

    def one_group(group, unused):
        start = pl.multiple_of(group * rows, rows)
        here = targets[pl.ds(start, rows), :]
        own = [jnp.broadcast_to(here[:, k : k + 1], (rows, 128)) for k in range(6)]

        def one_chunk(chunk, carry):
            sums = list(carry)
            for part in range(stars // 128):
                there = [
                    jnp.broadcast_to(sources[chunk, k : k + 1, part * 128 : part * 128 + 128], (rows, 128))
                    for k in range(7)
                ]
                r = [there[k] - own[k] for k in range(3)]
                u = [there[k + 3] - own[k + 3] for k in range(3)]
                q = r[0] * r[0] + r[1] * r[1] + r[2] * r[2] + SOFTENING
                s = r[0] * u[0] + r[1] * u[1] + r[2] * u[2]
                inverse = lax.rsqrt(q)
                squared = inverse * inverse
                weight = there[6] * inverse * squared
                radial = s * squared
                for k in range(3):
                    pull = weight * r[k]
                    sums[k] = sums[k] + pull
                    sums[k + 3] = sums[k + 3] + weight * u[k]
                    sums[k + 6] = sums[k + 6] + radial * pull
            return tuple(sums)

        zero = jnp.zeros((rows, 128), jnp.float32)
        sums = lax.fori_loop(0, sources.shape[0], one_chunk, (zero,) * 9)
        accel = [jnp.sum(sums[k], 1, keepdims=True) for k in range(3)]
        jerk = [jnp.sum(sums[k + 3] - 3.0 * sums[k + 6], 1, keepdims=True) for k in range(3)]
        result[pl.ds(start, rows), :] = jnp.concatenate(accel + jerk + accel[:2], 1)
        return unused

    lax.fori_loop(0, targets.shape[0] // rows, one_group, 0)


def local(position, velocity, accel_old, jerk_old, mass, elapsed, active_index):
    stars, active = position.shape[1], active_index.shape[0]
    blocks, members = lax.axis_size("blk"), lax.axis_size("grp")
    device = lax.axis_index("blk") * members + lax.axis_index("grp")
    offsets = active_index - device * stars
    f32 = jnp.float32
    predicted, sources, targets = pl.pallas_call(
        prologue_kernel,
        out_shape=(
            jax.ShapeDtypeStruct((6, stars), f32),
            jax.ShapeDtypeStruct((blocks, 8, stars), f32),
            jax.ShapeDtypeStruct((members, active, 8), f32),
        ),
        name="prologue",
    )(offsets[:, None], position, velocity, accel_old, jerk_old, mass[None], elapsed[None])
    targets = lax.all_to_all(targets, "grp", 0, 0, tiled=True)
    sources = lax.all_to_all(sources, "blk", 0, 0, tiled=True)
    result = pl.pallas_call(
        interact_kernel,
        out_shape=jax.ShapeDtypeStruct((members * active, 8), f32),
        name="interact",
    )(sources, targets.reshape(members * active, 8))
    parts = lax.all_to_all(result.reshape(members, active, 8), "grp", 0, 0, tiled=True)
    owned = parts.sum(axis=0).T
    return (predicted, owned[0:3], owned[3:6])


def solution(mesh):
    whole = P(None, ("blk", "grp"))
    flat = P(("blk", "grp"))
    return jax.shard_map(
        local,
        mesh=mesh,
        in_specs=(whole, whole, whole, whole, flat, flat, flat),
        out_specs=(whole, whole, whole),
        check_vma=False,
    )
```

```python
import jax
import jax.numpy as jnp
from jax import lax
from jax.experimental import pallas as pl
from jax.experimental.pallas import tpu as pltpu
from jax.sharding import PartitionSpec as P

SOFTENING = 0.0001
LANES = 128
STEP = 256
F32 = jnp.float32
BF16 = jnp.bfloat16


def in_three(value):
    high = value.astype(BF16)
    rest = value - high.astype(F32)
    middle = rest.astype(BF16)
    low = (rest - middle.astype(F32)).astype(BF16)
    return high, middle, low


def lane_iota(shape):
    return lax.broadcasted_iota(jnp.int32, shape, len(shape) - 1)


def row_iota(shape):
    return lax.broadcasted_iota(jnp.int32, shape, 0)


def prologue_kernel(first, active_index, position, velocity, accel_old, jerk_old, mass, elapsed, predicted, sources, targets):
    active, stars = active_index.shape[1], position.shape[1]
    step_row = elapsed[...]
    half = step_row * step_row * 0.5
    sixth = half * step_row * (1.0 / 3.0)
    new_position = position[...] + step_row * velocity[...] + half * accel_old[...] + sixth * jerk_old[...]
    new_velocity = velocity[...] + step_row * accel_old[...] + half * jerk_old[...]
    predicted[0:3, :] = new_position
    predicted[3:6, :] = new_velocity
    everything = jnp.concatenate([new_position, new_velocity, mass[...], jnp.ones_like(step_row)], 0)
    for copy in range(sources.shape[0]):
        sources[copy] = everything
    offsets = active_index[...] - first[0]
    chosen = jnp.where(row_iota((stars, active)) == offsets, 1.0, 0.0).astype(BF16)
    high, middle, low = in_three(everything)
    dot = lambda piece: jnp.dot(piece, chosen, preferred_element_type=F32)
    picked = (dot(high) + dot(middle)) + dot(low)
    picked = jnp.concatenate([picked, jnp.zeros((8, LANES - active), F32)], 1)
    spread = pltpu.roll(picked, 0, 1, stride=active, stride_axis=0)
    line = jnp.sum(spread, 0, keepdims=True)
    targets[...] = jnp.broadcast_to(line, targets.shape)


def unpack_targets(message, active):
    rows = []
    for k in range(6):
        pieces = []
        for group in range(message.shape[0] // 8):
            part = message[group * 8 : group * 8 + 8, :]
            turned = pltpu.roll(part, (LANES - k * active) % LANES, 1) if k else part
            turned = pltpu.roll(turned, 0, 1, stride=active, stride_axis=0)
            kept = jnp.where(lane_iota((8, LANES)) // active == row_iota((8, LANES)), turned, 0.0)
            pieces.append(jnp.sum(kept, 0, keepdims=True))
        rows.append(jnp.concatenate(pieces, 1))
    return rows


def pack_results(rows, active, result):
    stacked = jnp.concatenate(rows + rows[:2], 0)
    piece, row = lane_iota((8, LANES)) // active, row_iota((8, LANES))
    for group in range(result.shape[0] // 8):
        part = stacked[:, group * LANES : group * LANES + LANES]
        total = jnp.zeros((8, LANES), F32)
        for shift in range(8):
            turned = pltpu.roll(part, shift * active, 1) if shift else part
            line = jnp.sum(jnp.where(piece == row, turned, 0.0), 0, keepdims=True)
            total = jnp.where((piece - row) % 8 == shift, jnp.broadcast_to(line, (8, LANES)), total)
        result[group * 8 : group * 8 + 8, :] = total


def radial_features(state, first_order):
    row = row_iota(state.shape)
    grid = jnp.where(row < 3, 1.5 * 2.0**20, 1.5 * 2.0**14)
    coarse = (state + grid) - grid
    fine = state - coarse
    exact = lambda value: value.astype(BF16).astype(F32)
    top = exact(coarse)
    bottom = coarse - top
    first = exact(fine)
    second = exact(fine - first)
    third = fine - first - second
    line = lambda value, k: value[k : k + 1]
    both = [line(coarse, k) * line(coarse, k + 3) for k in range(3)]
    whole = both[0] + both[1] + both[2]
    mixed = [line(coarse, k) * line(fine, k + 3) + line(fine, k) * line(state, k + 3) for k in range(3)]
    part = mixed[0] + mixed[1] + mixed[2]
    pieces = []
    for value in (whole, part):
        high = exact(value)
        middle = exact(value - high)
        pieces.append((high, middle, value - high - middle))
    pick = lambda upper, lower: jnp.where(row < 3, upper, lower)
    zero = jnp.zeros_like(state)
    groups = [
        (top, pieces[0][0]),
        (pick(top, bottom), pieces[0][1]),
        (zero, pieces[0][2]),
        (pick(top, first), pieces[1][0]),
        (pick(top, second), pieces[1][1]),
        (pick(first, top), pieces[1][2]),
        (pick(first, bottom), None),
        (first, None),
        (pick(second, top), None),
        (pick(second, bottom), None),
        (pick(third, top), None),
    ]
    rows = []
    for value, extra in groups:
        if not first_order:
            value = -jnp.concatenate([value[3:6], value[0:3], value[6:8]], 0)
        if extra is None:
            value = jnp.where(row < 6, value, 0.0)
        else:
            wide = jnp.broadcast_to(extra, value.shape)
            value = jnp.where(row < 6, value, jnp.where(row == (6 if first_order else 7), wide, 1.0))
        rows.append(value)
    rows += [zero] * (16 - len(rows))
    return jnp.concatenate(rows, 0)


def spread_columns(block, spread, count):
    columns = block.T
    for row in range(0, columns.shape[0], 8):
        for k in range(count):
            spread[k, row : row + 8, :] = jnp.broadcast_to(columns[row : row + 8, k : k + 1], (8, LANES))


def own_kernel(sources, message, result, spread, *, active):
    stars = sources.shape[1]
    spread_columns(sources[...], spread, 7)
    lines = unpack_targets(message[...], active)
    wide = message.shape[0] * active
    total = []
    for group in range(wide // LANES):
        own = [jnp.broadcast_to(line[:, group * LANES : group * LANES + LANES], (8, LANES)) for line in lines]

        def one(step, carry):
            sums = list(carry)
            for part in range(4):
                start = pl.multiple_of(step * 32, 32) + part * 8
                there = [spread[k, pl.ds(start, 8), :] for k in range(7)]
                r = [there[k] - own[k] for k in range(3)]
                u = [there[k + 3] - own[k + 3] for k in range(3)]
                q = r[0] * r[0] + r[1] * r[1] + r[2] * r[2] + SOFTENING
                s = r[0] * u[0] + r[1] * u[1] + r[2] * u[2]
                inverse = lax.rsqrt(q)
                squared = inverse * inverse
                weight = there[6] * inverse * squared
                radial = s * squared
                for k in range(3):
                    pull = weight * r[k]
                    sums[k] = sums[k] + pull
                    sums[k + 3] = sums[k + 3] + weight * u[k]
                    sums[k + 6] = sums[k + 6] + radial * pull
            return tuple(sums)

        sums = lax.fori_loop(0, stars // 32, one, (jnp.zeros((8, LANES), F32),) * 9)
        ready = list(sums[:3]) + [sums[k + 3] - 3.0 * sums[k + 6] for k in range(3)]
        total.append([jnp.sum(value, 0, keepdims=True) for value in ready])
    rows = [jnp.concatenate([part[k] for part in total], 1) for k in range(6)]
    result[...] = jnp.concatenate(rows + rows[:2], 0)


def main_kernel(block, sources, message, own_result, result, spread, target_rows, target_side, sum_w, sum_d, *, active):
    blocks, stars = sources.shape[0], sources.shape[2]
    wide = message.shape[0] * active
    groups = wide // LANES
    lines = unpack_targets(message[...], active)
    target_side[...] = radial_features(jnp.concatenate(lines + lines[:2], 0), False).astype(BF16)
    middle_of = lambda line: 0.5 * (jnp.min(line, 1, keepdims=True) + jnp.max(line, 1, keepdims=True))
    centers = [middle_of(line) for line in lines]
    center = jnp.concatenate(centers + [jnp.zeros((2, 1), F32)], 0)
    for k, row in enumerate(lines):
        for g in range(groups):
            target_rows[g, k * 8 : k * 8 + 8, :] = jnp.broadcast_to(row[:, g * LANES : g * LANES + LANES], (8, LANES))
    sum_w[...] = jnp.zeros(sum_w.shape, F32)
    sum_d[...] = jnp.zeros(sum_d.shape, F32)

    def one_block(turn, unused):
        chunk = lax.rem(block[0] + 1 + turn, blocks)
        here = sources[chunk]
        scaled = (here - center) * here[6:7]
        high, middle, low = in_three(scaled)
        stacked = jnp.concatenate([high.astype(F32), middle.astype(F32), low.astype(F32), jnp.zeros_like(scaled)], 0).astype(BF16)
        source_side = radial_features(here, True).T.astype(BF16)
        for step in range(stars // STEP):
            spread_columns(here[:, step * STEP : step * STEP + STEP], spread.at[step], 3)
            part = stacked[:, step * STEP : step * STEP + STEP]
            left = jnp.concatenate([part, part], 1)
            for half in range(groups // 2):
                lanes = slice(half * 2 * LANES, half * 2 * LANES + 2 * LANES)
                products = jnp.dot(
                    source_side[step * STEP : step * STEP + STEP], target_side[:, lanes], preferred_element_type=F32
                )
                full = [[], [], [], []]
                for row in range(0, STEP, 16):
                    across = [[], [], [], []]
                    for g in (2 * half, 2 * half + 1):
                        own = [target_rows[g, k * 8 : k * 8 + 8, :] for k in range(3)]
                        at_lane = (g - 2 * half) * LANES
                        both_w, both_d = [], []
                        for sub in range(2):
                            top = row + sub * 8
                            there = [spread[step, k, top : top + 8, :] for k in range(3)]
                            r = [there[k] - own[k] for k in range(3)]
                            q = r[0] * r[0] + r[1] * r[1] + (r[2] * r[2] + SOFTENING)
                            s = products[top : top + 8, at_lane : at_lane + LANES]
                            inverse = lax.rsqrt(q)
                            squared = inverse * inverse
                            weight = inverse * squared
                            both_w.append(weight)
                            both_d.append(weight * (s * squared))
                        for at, both in ((0, both_w), (2, both_d)):
                            value = jnp.concatenate(both, 0)
                            upper = value.astype(BF16)
                            across[at].append(upper)
                            across[at + 1].append((value - upper.astype(F32)).astype(BF16))
                    for at in range(4):
                        full[at].append(jnp.concatenate(across[at], 1))
                right_w = jnp.concatenate(full[0] + full[1], 0)
                right_d = jnp.concatenate(full[2] + full[3], 0)
                sum_w[:, lanes] += jnp.dot(left, right_w, preferred_element_type=F32)
                sum_d[:, lanes] += jnp.dot(left, right_d, preferred_element_type=F32)
        return unused

    lax.fori_loop(0, blocks - 1, one_block, 0)
    total_w = sum_w[0:8] + (sum_w[8:16] + sum_w[16:24])
    total_d = sum_d[0:8] + (sum_d[8:16] + sum_d[16:24])
    here = [jnp.concatenate([target_rows[g, k * 8 : k * 8 + 1, :] for g in range(groups)], 1) for k in range(6)]
    here = [value - middle for value, middle in zip(here, centers)]
    rows = []
    for k in range(3):
        rows.append(own_result[k : k + 1] + (total_w[k : k + 1] - here[k] * total_w[7:8]))
    for k in range(3):
        straight = total_w[k + 3 : k + 4] - here[k + 3] * total_w[7:8]
        inward = total_d[k : k + 1] - here[k] * total_d[7:8]
        rows.append(own_result[k + 3 : k + 4] + (straight - 3.0 * inward))
    pack_results(rows, active, result)


def final_kernel(parts, accel, jerk, *, active):
    line = jnp.broadcast_to(jnp.sum(parts[...], 0, keepdims=True), (8, LANES))
    for k in range(6):
        turned = pltpu.roll(line, LANES - k * active, 1) if k else line
        (accel if k < 3 else jerk)[k % 3 : k % 3 + 1, :] = turned[k : k + 1, :active]


def shape(*lengths):
    return jax.ShapeDtypeStruct(lengths, F32)


def local(position, velocity, accel_old, jerk_old, mass, elapsed, active_index):
    stars, active = position.shape[1], active_index.shape[0]
    blocks, members = lax.axis_size("blk"), lax.axis_size("grp")
    block = lax.axis_index("blk")
    first = ((block * members + lax.axis_index("grp")) * stars)[None]
    scalar = pl.BlockSpec(memory_space=pltpu.SMEM)
    vector = pl.BlockSpec(memory_space=pltpu.VMEM)
    predicted, sources, targets = pl.pallas_call(
        prologue_kernel,
        out_shape=(shape(6, stars), shape(blocks, 8, stars), shape(members, LANES)),
        in_specs=[scalar] + [vector] * 7,
        name="prologue",
    )(first, active_index[None], position, velocity, accel_old, jerk_old, mass[None], elapsed[None])
    message = lax.all_to_all(targets, "grp", 0, 0, tiled=True)
    gathered = lax.all_to_all(sources, "blk", 0, 0, tiled=True)
    result = interact(block[None], sources[0], gathered, message, active)
    parts = lax.all_to_all(result, "grp", 0, 0, tiled=True)
    accel, jerk = pl.pallas_call(
        lambda *refs: final_kernel(*refs, active=active), out_shape=(shape(3, active), shape(3, active)), name="final"
    )(parts)
    return (predicted, accel, jerk)


def interact(block, mine, gathered, message, active):
    stars, wide = mine.shape[1], message.shape[0] * active
    scalar = pl.BlockSpec(memory_space=pltpu.SMEM)
    vector = pl.BlockSpec(memory_space=pltpu.VMEM)
    own_result = pl.pallas_call(
        lambda *refs: own_kernel(*refs, active=active),
        out_shape=shape(8, wide),
        scratch_shapes=[pltpu.VMEM((7, stars, LANES), F32)],
        name="own",
    )(mine, message)
    steps = stars // STEP
    return pl.pallas_call(
        lambda *refs: main_kernel(*refs, active=active),
        out_shape=shape(message.shape[0], LANES),
        in_specs=[scalar, vector, vector, vector],
        scratch_shapes=[
            pltpu.VMEM((steps, 3, STEP, LANES), F32),
            pltpu.VMEM((wide // LANES, 48, LANES), F32),
            pltpu.VMEM((LANES, wide), BF16),
            pltpu.VMEM((32, wide), F32),
            pltpu.VMEM((32, wide), F32),
        ],
        name="interact",
    )(block, gathered, message, own_result)


def solution(mesh):
    whole = P(None, ("blk", "grp"))
    flat = P(("blk", "grp"))
    return jax.shard_map(
        local,
        mesh=mesh,
        in_specs=(whole, whole, whole, whole, flat, flat, flat),
        out_specs=(whole, whole, whole),
        check_vma=False,
    )
```

```python
import jax
import jax.numpy as jnp
from jax import lax
from jax.experimental import pallas as pl
from jax.experimental.pallas import tpu as pltpu
from jax.sharding import PartitionSpec as P

SOFTENING = 0.0001
SQUARE_HALVES = ()
LANES = 128
STEP = 256
F32 = jnp.float32
BF16 = jnp.bfloat16


def in_three(value):
    high = value.astype(BF16)
    rest = value - high.astype(F32)
    middle = rest.astype(BF16)
    low = (rest - middle.astype(F32)).astype(BF16)
    return high, middle, low


def lane_iota(shape):
    return lax.broadcasted_iota(jnp.int32, shape, len(shape) - 1)


def row_iota(shape):
    return lax.broadcasted_iota(jnp.int32, shape, 0)


def prologue_kernel(first, active_index, position, velocity, accel_old, jerk_old, mass, elapsed, predicted, sources, targets):
    active, stars = active_index.shape[1], position.shape[1]
    step_row = elapsed[...]
    half = step_row * step_row * 0.5
    sixth = half * step_row * (1.0 / 3.0)
    new_position = position[...] + step_row * velocity[...] + half * accel_old[...] + sixth * jerk_old[...]
    new_velocity = velocity[...] + step_row * accel_old[...] + half * jerk_old[...]
    predicted[0:3, :] = new_position
    predicted[3:6, :] = new_velocity
    everything = jnp.concatenate([new_position, jnp.ones_like(step_row), new_velocity, mass[...]], 0)
    for copy in range(sources.shape[0]):
        sources[copy] = everything
    offsets = active_index[...] - first[0]
    chosen = jnp.where(row_iota((stars, active)) == offsets, 1.0, 0.0).astype(BF16)
    high, middle, low = in_three(everything)
    dot = lambda piece: jnp.dot(piece, chosen, preferred_element_type=F32)
    picked = (dot(high) + dot(middle)) + dot(low)
    picked = jnp.concatenate([picked[0:3], picked[4:7], picked[0:2]], 0)
    picked = jnp.concatenate([picked, jnp.zeros((8, LANES - active), F32)], 1)
    spread = pltpu.roll(picked, 0, 1, stride=active, stride_axis=0)
    line = jnp.sum(spread, 0, keepdims=True)
    targets[...] = jnp.broadcast_to(line, targets.shape)


def unpack_targets(message, active):
    rows = []
    for k in range(6):
        pieces = []
        for group in range(message.shape[0] // 8):
            part = message[group * 8 : group * 8 + 8, :]
            turned = pltpu.roll(part, (LANES - k * active) % LANES, 1) if k else part
            turned = pltpu.roll(turned, 0, 1, stride=active, stride_axis=0)
            kept = jnp.where(lane_iota((8, LANES)) // active == row_iota((8, LANES)), turned, 0.0)
            pieces.append(jnp.sum(kept, 0, keepdims=True))
        rows.append(jnp.concatenate(pieces, 1))
    return rows


def pack_results(rows, active, result):
    stacked = jnp.concatenate(rows + rows[:2], 0)
    piece, row = lane_iota((8, LANES)) // active, row_iota((8, LANES))
    for group in range(result.shape[0] // 8):
        part = stacked[:, group * LANES : group * LANES + LANES]
        total = jnp.zeros((8, LANES), F32)
        for shift in range(8):
            turned = pltpu.roll(part, shift * active, 1) if shift else part
            line = jnp.sum(jnp.where(piece == row, turned, 0.0), 0, keepdims=True)
            total = jnp.where((piece - row) % 8 == shift, jnp.broadcast_to(line, (8, LANES)), total)
        result[group * 8 : group * 8 + 8, :] = total


def exact(value):
    return value.astype(BF16).astype(F32)


def three_parts(value):
    high = exact(value)
    rest = value - high
    middle = exact(rest)
    return high, middle, rest - middle


def halves(upper, lower):
    return jnp.where(row_iota(upper.shape) < 4, upper, lower)


def swap(value):
    return pltpu.roll(value, 4, 0)


def with_one(value):
    return jnp.where(row_iota(value.shape) == 3, 1.0, value)


def constant_groups(product, mixed):
    p, m = three_parts(product), three_parts(mixed)
    return with_one(halves(p[0], p[1])), with_one(halves(p[2], m[0])), halves(m[1], m[2])


def radial_parts(state):
    grid = jnp.where(row_iota(state.shape) < 4, 1.5 * 2.0**20, 1.5 * 2.0**14)
    coarse = (state + grid) - grid
    fine = state - coarse
    top = exact(coarse)
    bottom = coarse - top
    first, second, third = three_parts(fine)
    product = coarse * swap(coarse)
    cross = coarse * swap(fine)
    mixed = (cross + swap(cross)) + fine * swap(fine)
    before = [top, halves(top, bottom)]
    after = [halves(top, first), halves(top, second), halves(first, top), halves(first, bottom), first]
    after += [halves(second, top), halves(second, bottom), halves(third, top)]
    return before, after, product, mixed


def square_parts(state):
    both = halves(state, swap(state))
    coarse = (both + 1.5 * 2.0**17) - 1.5 * 2.0**17
    fine = both - coarse
    upper = (coarse + 1.5 * 2.0**21) - 1.5 * 2.0**21
    lower = coarse - upper
    first = exact(fine)
    return upper, lower, first, fine - first, coarse * coarse, fine * ((coarse + coarse) + fine)


def stack(groups):
    return jnp.concatenate(groups + [jnp.zeros_like(groups[0])] * (16 - len(groups)), 0)


def source_features(state):
    before, after, product, mixed = radial_parts(state)
    one, two, last = constant_groups(product, mixed)
    radial = stack(before + [one, two] + after + [last])
    upper, lower, first, second, product, mixed = square_parts(state)
    one, two, last = constant_groups(product, mixed)
    a, b = halves(upper, lower), halves(first, second)
    return radial, stack([a, a, one, two, a, a, b, b, b, b, last])


def target_features(state):
    row = row_iota(state.shape)
    inside = (row != 3) & (row != 7)
    ones = jnp.where(inside, 1.0, 0.0)

    def constants(product, mixed, extra):
        add = lambda value: value[0:1] + value[1:2] + value[2:3]
        return three_parts(add(product)) + three_parts(add(mixed) + extra)

    def filled(group, value):
        group = jnp.where(inside, group, 0.0)
        return group if value is None else jnp.where(row == 3, jnp.broadcast_to(value, group.shape), group)

    before, after, product, mixed = radial_parts(state)
    c = constants(product, mixed, 0.0)
    flip = lambda group: -swap(group)
    radial = [filled(flip(before[0]), c[0]), filled(flip(before[1]), c[1]), filled(ones, c[2]), filled(ones, c[3])]
    radial += [filled(flip(after[0]), c[4]), filled(flip(after[1]), c[5])] + [filled(flip(group), None) for group in after[2:]]
    upper, lower, first, second, product, mixed = square_parts(state)
    c = constants(product, mixed, SOFTENING)
    pair = lambda a, b: -2.0 * halves(a, b)
    square = [filled(pair(upper, lower), c[0]), filled(pair(lower, upper), c[1]), filled(ones, c[2]), filled(ones, c[3])]
    square += [filled(pair(first, first), c[4]), filled(pair(second, second), c[5])]
    square += [filled(pair(a, b), None) for a, b in ((upper, upper), (lower, lower), (first, first), (second, 0.0 * second))]
    return stack(radial + [ones]), stack(square + [ones])


def spread_columns(block, spread, picks):
    columns = block.T
    for row in range(0, columns.shape[0], 8):
        for k, pick in enumerate(picks):
            spread[k, row : row + 8, :] = jnp.broadcast_to(columns[row : row + 8, pick : pick + 1], (8, LANES))


def own_kernel(sources, message, result, spread, *, active):
    stars = sources.shape[1]
    spread_columns(sources[...], spread, (0, 1, 2, 4, 5, 6, 7))
    lines = unpack_targets(message[...], active)
    wide = message.shape[0] * active
    total = []
    for group in range(wide // LANES):
        own = [jnp.broadcast_to(line[:, group * LANES : group * LANES + LANES], (8, LANES)) for line in lines]

        def one(step, carry):
            sums = list(carry)
            for part in range(4):
                start = pl.multiple_of(step * 32, 32) + part * 8
                there = [spread[k, pl.ds(start, 8), :] for k in range(7)]
                r = [there[k] - own[k] for k in range(3)]
                u = [there[k + 3] - own[k + 3] for k in range(3)]
                q = r[0] * r[0] + r[1] * r[1] + r[2] * r[2] + SOFTENING
                s = r[0] * u[0] + r[1] * u[1] + r[2] * u[2]
                inverse = lax.rsqrt(q)
                squared = inverse * inverse
                weight = there[6] * inverse * squared
                radial = s * squared
                for k in range(3):
                    pull = weight * r[k]
                    sums[k] = sums[k] + pull
                    sums[k + 3] = sums[k + 3] + weight * u[k]
                    sums[k + 6] = sums[k + 6] + radial * pull
            return tuple(sums)

        sums = lax.fori_loop(0, stars // 32, one, (jnp.zeros((8, LANES), F32),) * 9)
        ready = list(sums[:3]) + [sums[k + 3] - 3.0 * sums[k + 6] for k in range(3)]
        total.append([jnp.sum(value, 0, keepdims=True) for value in ready])
    rows = [jnp.concatenate([part[k] for part in total], 1) for k in range(6)]
    result[...] = jnp.concatenate(rows + rows[:2], 0)


def main_kernel(block, sources, message, own_result, result, spread, target_rows, radial_side, square_side, sum_w, sum_d, *, active):
    blocks, stars = sources.shape[0], sources.shape[2]
    wide = message.shape[0] * active
    groups = wide // LANES
    lines = unpack_targets(message[...], active)
    blank = jnp.zeros_like(lines[0])
    radial, square = target_features(jnp.concatenate(lines[:3] + [blank + 1.0] + lines[3:] + [blank], 0))
    radial_side[...] = radial.astype(BF16)
    square_side[...] = square.astype(BF16)
    middle_of = lambda line: 0.5 * (jnp.min(line, 1, keepdims=True) + jnp.max(line, 1, keepdims=True))
    centers = [middle_of(line) for line in lines]
    nothing = jnp.zeros((1, 1), F32)
    center = jnp.concatenate(centers[:3] + [nothing] + centers[3:] + [nothing], 0)
    for k, row in enumerate(lines[:3]):
        for g in range(groups):
            target_rows[g, k * 8 : k * 8 + 8, :] = jnp.broadcast_to(row[:, g * LANES : g * LANES + LANES], (8, LANES))
    sum_w[...] = jnp.zeros(sum_w.shape, F32)
    sum_d[...] = jnp.zeros(sum_d.shape, F32)

    def one_block(turn, unused):
        chunk = lax.rem(block[0] + 1 + turn, blocks)
        here = sources[chunk]
        scaled = (here - center) * here[7:8]
        high, middle, low = in_three(scaled)
        stacked = jnp.concatenate([high.astype(F32), middle.astype(F32), low.astype(F32), jnp.zeros_like(scaled)], 0).astype(BF16)
        radial, square = source_features(here)
        radial = radial.T.astype(BF16)
        square = square.T.astype(BF16)
        for step in range(stars // STEP):
            spread_columns(here[:, step * STEP : step * STEP + STEP], spread.at[step], (0, 1, 2))
            part = stacked[:, step * STEP : step * STEP + STEP]
            left = jnp.concatenate([part, part], 1)
            for half in range(groups // 2):
                lanes = slice(half * 2 * LANES, half * 2 * LANES + 2 * LANES)
                some = slice(step * STEP, step * STEP + STEP)
                products = jnp.dot(radial[some], radial_side[:, lanes], preferred_element_type=F32)
                by_product = half in SQUARE_HALVES
                if by_product:
                    squares = jnp.dot(square[some], square_side[:, lanes], preferred_element_type=F32)
                full = [[], [], [], []]
                for row in range(0, STEP, 16):
                    across = [[], [], [], []]
                    for g in (2 * half, 2 * half + 1):
                        own = None if by_product else [target_rows[g, k * 8 : k * 8 + 8, :] for k in range(3)]
                        at_lane = (g - 2 * half) * LANES
                        both_w, both_d = [], []
                        for sub in range(2):
                            top = row + sub * 8
                            if by_product:
                                q = squares[top : top + 8, at_lane : at_lane + LANES]
                            else:
                                there = [spread[step, k, top : top + 8, :] for k in range(3)]
                                r = [there[k] - own[k] for k in range(3)]
                                q = r[0] * r[0] + r[1] * r[1] + (r[2] * r[2] + SOFTENING)
                            s = products[top : top + 8, at_lane : at_lane + LANES]
                            inverse = lax.rsqrt(q)
                            squared = inverse * inverse
                            weight = inverse * squared
                            both_w.append(weight)
                            both_d.append(weight * (s * squared))
                        for at, both in ((0, both_w), (2, both_d)):
                            value = jnp.concatenate(both, 0)
                            upper = value.astype(BF16)
                            across[at].append(upper)
                            across[at + 1].append((value - upper.astype(F32)).astype(BF16))
                    for at in range(4):
                        full[at].append(jnp.concatenate(across[at], 1))
                right_w = jnp.concatenate(full[0] + full[1], 0)
                right_d = jnp.concatenate(full[2] + full[3], 0)
                sum_w[:, lanes] += jnp.dot(left, right_w, preferred_element_type=F32)
                sum_d[:, lanes] += jnp.dot(left, right_d, preferred_element_type=F32)
        return unused

    lax.fori_loop(0, blocks - 1, one_block, 0, unroll=5)
    total_w = sum_w[0:8] + (sum_w[8:16] + sum_w[16:24])
    total_d = sum_d[0:8] + (sum_d[8:16] + sum_d[16:24])
    here = [value - middle for value, middle in zip(lines, centers)]
    rows = []
    for k in range(3):
        rows.append(own_result[k : k + 1] + (total_w[k : k + 1] - here[k] * total_w[3:4]))
    for k in range(3):
        straight = total_w[k + 4 : k + 5] - here[k + 3] * total_w[3:4]
        inward = total_d[k : k + 1] - here[k] * total_d[3:4]
        rows.append(own_result[k + 3 : k + 4] + (straight - 3.0 * inward))
    pack_results(rows, active, result)


def final_kernel(parts, accel, jerk, *, active):
    line = jnp.broadcast_to(jnp.sum(parts[...], 0, keepdims=True), (8, LANES))
    for k in range(6):
        turned = pltpu.roll(line, LANES - k * active, 1) if k else line
        (accel if k < 3 else jerk)[k % 3 : k % 3 + 1, :] = turned[k : k + 1, :active]


def shape(*lengths):
    return jax.ShapeDtypeStruct(lengths, F32)


def local(position, velocity, accel_old, jerk_old, mass, elapsed, active_index):
    stars, active = position.shape[1], active_index.shape[0]
    blocks, members = lax.axis_size("blk"), lax.axis_size("grp")
    block = lax.axis_index("blk")
    first = ((block * members + lax.axis_index("grp")) * stars)[None]
    scalar = pl.BlockSpec(memory_space=pltpu.SMEM)
    vector = pl.BlockSpec(memory_space=pltpu.VMEM)
    predicted, sources, targets = pl.pallas_call(
        prologue_kernel,
        out_shape=(shape(6, stars), shape(blocks, 8, stars), shape(members, LANES)),
        in_specs=[scalar] + [vector] * 7,
        name="prologue",
    )(first, active_index[None], position, velocity, accel_old, jerk_old, mass[None], elapsed[None])
    message = lax.all_to_all(targets, "grp", 0, 0, tiled=True)
    gathered = lax.all_to_all(sources, "blk", 0, 0, tiled=True)
    result = interact(block[None], sources[0], gathered, message, active)
    parts = lax.all_to_all(result, "grp", 0, 0, tiled=True)
    accel, jerk = pl.pallas_call(
        lambda *refs: final_kernel(*refs, active=active), out_shape=(shape(3, active), shape(3, active)), name="final"
    )(parts)
    return (predicted, accel, jerk)


def interact(block, mine, gathered, message, active):
    stars, wide = mine.shape[1], message.shape[0] * active
    scalar = pl.BlockSpec(memory_space=pltpu.SMEM)
    vector = pl.BlockSpec(memory_space=pltpu.VMEM)
    own_result = pl.pallas_call(
        lambda *refs: own_kernel(*refs, active=active),
        out_shape=shape(8, wide),
        scratch_shapes=[pltpu.VMEM((7, stars, LANES), F32)],
        name="own",
    )(mine, message)
    steps = stars // STEP
    return pl.pallas_call(
        lambda *refs: main_kernel(*refs, active=active),
        out_shape=shape(message.shape[0], LANES),
        in_specs=[scalar, vector, vector, vector],
        scratch_shapes=[
            pltpu.VMEM((steps, 3, STEP, LANES), F32),
            pltpu.VMEM((wide // LANES, 24, LANES), F32),
            pltpu.VMEM((LANES, wide), BF16),
            pltpu.VMEM((LANES, wide), BF16),
            pltpu.VMEM((32, wide), F32),
            pltpu.VMEM((32, wide), F32),
        ],
        name="interact",
    )(block, gathered, message, own_result)


def solution(mesh):
    whole = P(None, ("blk", "grp"))
    flat = P(("blk", "grp"))
    return jax.shard_map(
        local,
        mesh=mesh,
        in_specs=(whole, whole, whole, whole, flat, flat, flat),
        out_specs=(whole, whole, whole),
        check_vma=False,
    )
```

```python
import jax
import jax.numpy as jnp
from jax import lax
from jax.experimental import pallas as pl
from jax.experimental.pallas import tpu as pltpu
from jax.sharding import PartitionSpec as P

SOFTENING = 0.0001
LANES = 128
STEP = 256
F32 = jnp.float32
BF16 = jnp.bfloat16


def in_three(value):
    high = value.astype(BF16)
    rest = value - high.astype(F32)
    middle = rest.astype(BF16)
    low = (rest - middle.astype(F32)).astype(BF16)
    return high, middle, low


def lane_iota(shape):
    return lax.broadcasted_iota(jnp.int32, shape, len(shape) - 1)


def row_iota(shape):
    return lax.broadcasted_iota(jnp.int32, shape, 0)


def prologue_kernel(first, active_index, position, velocity, accel_old, jerk_old, mass, elapsed, predicted, sources, targets, mine):
    active, stars = active_index.shape[1], position.shape[1]
    step_row = elapsed[...]
    half = step_row * step_row * 0.5
    sixth = half * step_row * (1.0 / 3.0)
    new_position = position[...] + step_row * velocity[...] + half * accel_old[...] + sixth * jerk_old[...]
    new_velocity = velocity[...] + step_row * accel_old[...] + half * jerk_old[...]
    predicted[0:3, :] = new_position
    predicted[3:6, :] = new_velocity
    everything = jnp.concatenate([new_position, jnp.ones_like(step_row), new_velocity, mass[...]], 0)
    mine[...] = everything
    for copy in range(sources.shape[0]):
        sources[copy] = everything
    offsets = active_index[...] - first[0]
    chosen = jnp.where(row_iota((stars, active)) == offsets, 1.0, 0.0).astype(BF16)
    high, middle, low = in_three(everything)
    dot = lambda piece: jnp.dot(piece, chosen, preferred_element_type=F32)
    picked = (dot(high) + dot(middle)) + dot(low)
    picked = jnp.concatenate([picked[0:3], picked[4:7], picked[0:2]], 0)
    picked = jnp.concatenate([picked, jnp.zeros((8, LANES - active), F32)], 1)
    spread = pltpu.roll(picked, 0, 1, stride=active, stride_axis=0)
    line = jnp.sum(spread, 0, keepdims=True)
    targets[...] = jnp.broadcast_to(line, targets.shape)


def unpack_targets(message, active):
    rows = []
    for k in range(6):
        pieces = []
        for group in range(message.shape[0] // 8):
            part = message[group * 8 : group * 8 + 8, :]
            turned = pltpu.roll(part, (LANES - k * active) % LANES, 1) if k else part
            turned = pltpu.roll(turned, 0, 1, stride=active, stride_axis=0)
            kept = jnp.where(lane_iota((8, LANES)) // active == row_iota((8, LANES)), turned, 0.0)
            pieces.append(jnp.sum(kept, 0, keepdims=True))
        rows.append(jnp.concatenate(pieces, 1))
    return rows


def pack_results(rows, active, result):
    stacked = jnp.concatenate(rows + rows[:2], 0)
    piece, row = lane_iota((8, LANES)) // active, row_iota((8, LANES))
    for group in range(result.shape[0] // 8):
        part = stacked[:, group * LANES : group * LANES + LANES]
        total = jnp.zeros((8, LANES), F32)
        for shift in range(8):
            turned = pltpu.roll(part, shift * active, 1) if shift else part
            line = jnp.sum(jnp.where(piece == row, turned, 0.0), 0, keepdims=True)
            total = jnp.where((piece - row) % 8 == shift, jnp.broadcast_to(line, (8, LANES)), total)
        result[group * 8 : group * 8 + 8, :] = total


def exact(value):
    return value.astype(BF16).astype(F32)


def three_parts(value):
    high = exact(value)
    rest = value - high
    middle = exact(rest)
    return high, middle, rest - middle


def halves(upper, lower):
    return jnp.where(row_iota(upper.shape) < 4, upper, lower)


def swap(value):
    return pltpu.roll(value, 4, 0)


def with_one(value):
    return jnp.where(row_iota(value.shape) == 3, 1.0, value)


def constant_groups(product, mixed):
    p, m = three_parts(product), three_parts(mixed)
    return with_one(halves(p[0], p[1])), with_one(halves(p[2], m[0])), halves(m[1], m[2])


def radial_parts(state):
    grid = jnp.where(row_iota(state.shape) < 4, 1.5 * 2.0**20, 1.5 * 2.0**14)
    coarse = (state + grid) - grid
    fine = state - coarse
    top = exact(coarse)
    bottom = coarse - top
    first, second, third = three_parts(fine)
    product = coarse * swap(coarse)
    cross = coarse * swap(fine)
    mixed = (cross + swap(cross)) + fine * swap(fine)
    before = [top, halves(top, bottom)]
    after = [halves(top, first), halves(top, second), halves(first, top), halves(first, bottom), first]
    after += [halves(second, top), halves(second, bottom), halves(third, top)]
    return before, after, product, mixed


def stack(groups):
    return jnp.concatenate(groups + [jnp.zeros_like(groups[0])] * (16 - len(groups)), 0)


def source_features(state):
    before, after, product, mixed = radial_parts(state)
    one, two, last = constant_groups(product, mixed)
    return stack(before + [one, two] + after + [last])


def target_features(state):
    row = row_iota(state.shape)
    inside = (row != 3) & (row != 7)
    ones = jnp.where(inside, 1.0, 0.0)

    def constants(product, mixed):
        add = lambda value: value[0:1] + value[1:2] + value[2:3]
        return three_parts(add(product)) + three_parts(add(mixed))

    def filled(group, value):
        group = jnp.where(inside, group, 0.0)
        return group if value is None else jnp.where(row == 3, jnp.broadcast_to(value, group.shape), group)

    before, after, product, mixed = radial_parts(state)
    c = constants(product, mixed)
    flip = lambda group: -swap(group)
    radial = [filled(flip(before[0]), c[0]), filled(flip(before[1]), c[1]), filled(ones, c[2]), filled(ones, c[3])]
    radial += [filled(flip(after[0]), c[4]), filled(flip(after[1]), c[5])] + [filled(flip(group), None) for group in after[2:]]
    return stack(radial + [ones])


def spread_columns(block, spread, picks):
    columns = block.T
    for row in range(0, columns.shape[0], 8):
        for k, pick in enumerate(picks):
            spread[k, row : row + 8, :] = jnp.broadcast_to(columns[row : row + 8, pick : pick + 1], (8, LANES))


def own_kernel(sources, message, result, here, center, target_rows, radial_side, spread, *, active):
    stars = sources.shape[1]
    spread_columns(sources[...], spread, (0, 1, 2, 4, 5, 6, 7))
    lines = unpack_targets(message[...], active)
    wide = message.shape[0] * active
    blank = jnp.zeros_like(lines[0])
    state = jnp.concatenate(lines[:3] + [blank + 1.0] + lines[3:] + [blank], 0)
    radial_side[...] = target_features(state).astype(BF16)
    middle = 0.5 * (jnp.min(state, 1, keepdims=True) + jnp.max(state, 1, keepdims=True))
    row = row_iota(state.shape)
    middle = jnp.where((row == 3) | (row == 7), 0.0, jnp.broadcast_to(middle, state.shape))
    here[...] = state - middle
    center[...] = middle[:, :LANES]
    for k, line in enumerate(lines[:3]):
        for g in range(wide // LANES):
            target_rows[g, k * 8 : k * 8 + 8, :] = jnp.broadcast_to(line[:, g * LANES : g * LANES + LANES], (8, LANES))
    total = []
    for group in range(wide // LANES):
        own = [jnp.broadcast_to(line[:, group * LANES : group * LANES + LANES], (8, LANES)) for line in lines]

        def one(step, carry):
            sums = list(carry)
            for part in range(4):
                start = pl.multiple_of(step * 32, 32) + part * 8
                there = [spread[k, pl.ds(start, 8), :] for k in range(7)]
                r = [there[k] - own[k] for k in range(3)]
                u = [there[k + 3] - own[k + 3] for k in range(3)]
                q = r[0] * r[0] + r[1] * r[1] + r[2] * r[2] + SOFTENING
                s = r[0] * u[0] + r[1] * u[1] + r[2] * u[2]
                inverse = lax.rsqrt(q)
                squared = inverse * inverse
                weight = there[6] * inverse * squared
                radial = s * squared
                for k in range(3):
                    pull = weight * r[k]
                    sums[k] = sums[k] + pull
                    sums[k + 3] = sums[k + 3] + weight * u[k]
                    sums[k + 6] = sums[k + 6] + radial * pull
            return tuple(sums)

        sums = lax.fori_loop(0, stars // 32, one, (jnp.zeros((8, LANES), F32),) * 9)
        ready = list(sums[:3]) + [sums[k + 3] - 3.0 * sums[k + 6] for k in range(3)]
        total.append([jnp.sum(value, 0, keepdims=True) for value in ready])
    rows = [jnp.concatenate([part[k] for part in total], 1) for k in range(6)]
    result[...] = jnp.concatenate(rows + rows[:2], 0)


def main_kernel(block, sources, own_result, here_rows, center, target_rows, radial_side, result, spread, sum_w, sum_d, *, active):
    blocks, stars = sources.shape[0], sources.shape[2]
    groups = here_rows.shape[1] // LANES
    sum_w[...] = jnp.zeros(sum_w.shape, F32)
    sum_d[...] = jnp.zeros(sum_d.shape, F32)

    def one_block(turn, unused):
        chunk = lax.rem(block[0] + 1 + turn, blocks)
        here = sources[chunk]
        scaled = (here - center[:, :1]) * here[7:8]
        high, middle, low = in_three(scaled)
        stacked = jnp.concatenate([high.astype(F32), middle.astype(F32), low.astype(F32), jnp.zeros_like(scaled)], 0).astype(BF16)
        radial = source_features(here).T.astype(BF16)
        for step in range(stars // STEP):
            spread_columns(here[:, step * STEP : step * STEP + STEP], spread.at[step], (0, 1, 2))
            part = stacked[:, step * STEP : step * STEP + STEP]
            left = jnp.concatenate([part, part], 1)
            for half in range(groups // 2):
                lanes = slice(half * 2 * LANES, half * 2 * LANES + 2 * LANES)
                some = slice(step * STEP, step * STEP + STEP)
                products = jnp.dot(radial[some], radial_side[:, lanes], preferred_element_type=F32)
                full = [[], [], [], []]
                for row in range(0, STEP, 16):
                    across = [[], [], [], []]
                    for g in (2 * half, 2 * half + 1):
                        own = [target_rows[g, k * 8 : k * 8 + 8, :] for k in range(3)]
                        at_lane = (g - 2 * half) * LANES
                        both_w, both_d = [], []
                        for sub in range(2):
                            top = row + sub * 8
                            there = [spread[step, k, top : top + 8, :] for k in range(3)]
                            r = [there[k] - own[k] for k in range(3)]
                            q = r[0] * r[0] + r[1] * r[1] + (r[2] * r[2] + SOFTENING)
                            s = products[top : top + 8, at_lane : at_lane + LANES]
                            inverse = lax.rsqrt(q)
                            squared = inverse * inverse
                            weight = inverse * squared
                            both_w.append(weight)
                            both_d.append(weight * (s * squared))
                        for at, both in ((0, both_w), (2, both_d)):
                            value = jnp.concatenate(both, 0)
                            upper = value.astype(BF16)
                            across[at].append(upper)
                            across[at + 1].append((value - upper.astype(F32)).astype(BF16))
                    for at in range(4):
                        full[at].append(jnp.concatenate(across[at], 1))
                right_w = jnp.concatenate(full[0] + full[1], 0)
                right_d = jnp.concatenate(full[2] + full[3], 0)
                sum_w[:, lanes] += jnp.dot(left, right_w, preferred_element_type=F32)
                sum_d[:, lanes] += jnp.dot(left, right_d, preferred_element_type=F32)
        return unused

    lax.fori_loop(0, blocks - 1, one_block, 0, unroll=5)
    total_w = sum_w[0:8] + (sum_w[8:16] + sum_w[16:24])
    total_d = sum_d[0:8] + (sum_d[8:16] + sum_d[16:24])
    here = [here_rows[k : k + 1] for k in (0, 1, 2, 4, 5, 6)]
    rows = []
    for k in range(3):
        rows.append(own_result[k : k + 1] + (total_w[k : k + 1] - here[k] * total_w[3:4]))
    for k in range(3):
        straight = total_w[k + 4 : k + 5] - here[k + 3] * total_w[3:4]
        inward = total_d[k : k + 1] - here[k] * total_d[3:4]
        rows.append(own_result[k + 3 : k + 4] + (straight - 3.0 * inward))
    pack_results(rows, active, result)


def final_kernel(parts, accel, jerk, *, active):
    line = jnp.broadcast_to(jnp.sum(parts[...], 0, keepdims=True), (8, LANES))
    for k in range(6):
        turned = pltpu.roll(line, LANES - k * active, 1) if k else line
        (accel if k < 3 else jerk)[k % 3 : k % 3 + 1, :] = turned[k : k + 1, :active]


def keep_near(value):
    return pltpu.with_memory_space_constraint(value, pltpu.VMEM)


def near(*lengths):
    return pltpu.VMEM(lengths, F32)


def shape(*lengths):
    return jax.ShapeDtypeStruct(lengths, F32)


def local(position, velocity, accel_old, jerk_old, mass, elapsed, active_index):
    stars, active = position.shape[1], active_index.shape[0]
    blocks, members = lax.axis_size("blk"), lax.axis_size("grp")
    block = lax.axis_index("blk")
    first = ((block * members + lax.axis_index("grp")) * stars)[None]
    scalar = pl.BlockSpec(memory_space=pltpu.SMEM)
    vector = pl.BlockSpec(memory_space=pltpu.VMEM)
    predicted, sources, targets, mine = pl.pallas_call(
        prologue_kernel,
        out_shape=(shape(6, stars), shape(blocks, 8, stars), near(members, LANES), near(8, stars)),
        in_specs=[scalar] + [vector] * 7,
        name="prologue",
    )(first, active_index[None], position, velocity, accel_old, jerk_old, mass[None], elapsed[None])
    message = lax.all_to_all(targets, "grp", 0, 0, tiled=True)
    gathered = lax.all_to_all(sources, "blk", 0, 0, tiled=True)
    result = interact(block[None], mine, gathered, message, active)
    parts = lax.all_to_all(result, "grp", 0, 0, tiled=True)
    parts = keep_near(parts)
    accel, jerk = pl.pallas_call(
        lambda *refs: final_kernel(*refs, active=active), out_shape=(shape(3, active), shape(3, active)), name="final"
    )(parts)
    return (predicted, accel, jerk)


def interact(block, mine, gathered, message, active):
    stars, wide = mine.shape[1], message.shape[0] * active
    groups = wide // LANES
    scalar = pl.BlockSpec(memory_space=pltpu.SMEM)
    vector = pl.BlockSpec(memory_space=pltpu.VMEM)
    mine, message = keep_near(mine), keep_near(message)
    prepared = pl.pallas_call(
        lambda *refs: own_kernel(*refs, active=active),
        out_shape=(near(8, wide), near(8, wide), near(8, LANES), near(groups, 24, LANES), pltpu.VMEM((LANES, wide), BF16)),
        scratch_shapes=[pltpu.VMEM((7, stars, LANES), F32)],
        name="own",
    )(mine, message)
    return pl.pallas_call(
        lambda *refs: main_kernel(*refs, active=active),
        out_shape=near(message.shape[0], LANES),
        in_specs=[scalar] + [vector] * 6,
        scratch_shapes=[
            pltpu.VMEM((stars // STEP, 3, STEP, LANES), F32),
            pltpu.VMEM((32, wide), F32),
            pltpu.VMEM((32, wide), F32),
        ],
        name="interact",
    )(block, keep_near(gathered), *[keep_near(value) for value in prepared])


def solution(mesh):
    whole = P(None, ("blk", "grp"))
    flat = P(("blk", "grp"))
    return jax.shard_map(
        local,
        mesh=mesh,
        in_specs=(whole, whole, whole, whole, flat, flat, flat),
        out_specs=(whole, whole, whole),
        check_vma=False,
    )
```

```python
import jax
import jax.numpy as jnp
from jax import lax
from jax.experimental import pallas as pl
from jax.experimental.pallas import tpu as pltpu
from jax.sharding import PartitionSpec as P

SOFTENING = 0.0001
LANES = 128
STEP = 256
F32 = jnp.float32
BF16 = jnp.bfloat16


def in_three(value):
    high = value.astype(BF16)
    rest = value - high.astype(F32)
    middle = rest.astype(BF16)
    low = (rest - middle.astype(F32)).astype(BF16)
    return high, middle, low


def lane_iota(shape):
    return lax.broadcasted_iota(jnp.int32, shape, len(shape) - 1)


def row_iota(shape):
    return lax.broadcasted_iota(jnp.int32, shape, 0)


def prologue_kernel(first, active_index, position, velocity, accel_old, jerk_old, mass, elapsed, predicted, sources, targets, mine):
    active, stars = active_index.shape[1], position.shape[1]
    step_row = elapsed[...]
    half = step_row * step_row * 0.5
    sixth = half * step_row * (1.0 / 3.0)
    new_position = position[...] + step_row * velocity[...] + half * accel_old[...] + sixth * jerk_old[...]
    new_velocity = velocity[...] + step_row * accel_old[...] + half * jerk_old[...]
    predicted[0:3, :] = new_position
    predicted[3:6, :] = new_velocity
    everything = jnp.concatenate([new_position, jnp.ones_like(step_row), new_velocity, mass[...]], 0)
    mine[...] = everything
    for copy in range(sources.shape[0]):
        sources[copy] = everything
    offsets = active_index[...] - first[0]
    chosen = jnp.where(row_iota((stars, active)) == offsets, 1.0, 0.0).astype(BF16)
    high, middle, low = in_three(everything)
    dot = lambda piece: jnp.dot(piece, chosen, preferred_element_type=F32)
    picked = (dot(high) + dot(middle)) + dot(low)
    picked = jnp.concatenate([picked[0:3], picked[4:7], picked[0:2]], 0)
    picked = jnp.concatenate([picked, jnp.zeros((8, LANES - active), F32)], 1)
    spread = pltpu.roll(picked, 0, 1, stride=active, stride_axis=0)
    line = jnp.sum(spread, 0, keepdims=True)
    targets[...] = jnp.broadcast_to(line, targets.shape)


def unpack_targets(message, active):
    rows = []
    for k in range(6):
        pieces = []
        for group in range(message.shape[0] // 8):
            part = message[group * 8 : group * 8 + 8, :]
            turned = pltpu.roll(part, (LANES - k * active) % LANES, 1) if k else part
            turned = pltpu.roll(turned, 0, 1, stride=active, stride_axis=0)
            kept = jnp.where(lane_iota((8, LANES)) // active == row_iota((8, LANES)), turned, 0.0)
            pieces.append(jnp.sum(kept, 0, keepdims=True))
        rows.append(jnp.concatenate(pieces, 1))
    return rows


def pack_results(rows, active, result):
    stacked = jnp.concatenate(rows + rows[:2], 0)
    piece, row = lane_iota((8, LANES)) // active, row_iota((8, LANES))
    for group in range(result.shape[0] // 8):
        part = stacked[:, group * LANES : group * LANES + LANES]
        total = jnp.zeros((8, LANES), F32)
        for shift in range(8):
            turned = pltpu.roll(part, shift * active, 1) if shift else part
            line = jnp.sum(jnp.where(piece == row, turned, 0.0), 0, keepdims=True)
            total = jnp.where((piece - row) % 8 == shift, jnp.broadcast_to(line, (8, LANES)), total)
        result[group * 8 : group * 8 + 8, :] = total


def exact(value):
    return value.astype(BF16).astype(F32)


def three_parts(value):
    high = exact(value)
    rest = value - high
    middle = exact(rest)
    return high, middle, rest - middle


def halves(upper, lower):
    return jnp.where(row_iota(upper.shape) < 4, upper, lower)


def swap(value):
    return pltpu.roll(value, 4, 0)


def with_one(value):
    return jnp.where(row_iota(value.shape) == 3, 1.0, value)


def constant_groups(product, mixed):
    p, m = three_parts(product), three_parts(mixed)
    return with_one(halves(p[0], p[1])), with_one(halves(p[2], m[0])), halves(m[1], m[2])


def radial_parts(state):
    grid = jnp.where(row_iota(state.shape) < 4, 1.5 * 2.0**20, 1.5 * 2.0**14)
    coarse = (state + grid) - grid
    fine = state - coarse
    top = exact(coarse)
    bottom = coarse - top
    first, second, third = three_parts(fine)
    product = coarse * swap(coarse)
    cross = coarse * swap(fine)
    mixed = (cross + swap(cross)) + fine * swap(fine)
    before = [top, halves(top, bottom)]
    after = [halves(top, first), halves(top, second), halves(first, top), halves(first, bottom), first]
    after += [halves(second, top), halves(second, bottom), halves(third, top)]
    return before, after, product, mixed


def stack(groups):
    return jnp.concatenate(groups + [jnp.zeros_like(groups[0])] * (16 - len(groups)), 0)


def source_features(state):
    before, after, product, mixed = radial_parts(state)
    one, two, last = constant_groups(product, mixed)
    return stack(before + [one, two] + after + [last])


def target_features(state):
    row = row_iota(state.shape)
    inside = (row != 3) & (row != 7)
    ones = jnp.where(inside, 1.0, 0.0)

    def constants(product, mixed):
        add = lambda value: value[0:1] + value[1:2] + value[2:3]
        return three_parts(add(product)) + three_parts(add(mixed))

    def filled(group, value):
        group = jnp.where(inside, group, 0.0)
        return group if value is None else jnp.where(row == 3, jnp.broadcast_to(value, group.shape), group)

    before, after, product, mixed = radial_parts(state)
    c = constants(product, mixed)
    flip = lambda group: -swap(group)
    radial = [filled(flip(before[0]), c[0]), filled(flip(before[1]), c[1]), filled(ones, c[2]), filled(ones, c[3])]
    radial += [filled(flip(after[0]), c[4]), filled(flip(after[1]), c[5])] + [filled(flip(group), None) for group in after[2:]]
    return stack(radial + [ones])


def spread_columns(block, spread, picks):
    columns = block.T
    for row in range(0, columns.shape[0], 8):
        for k, pick in enumerate(picks):
            spread[k, row : row + 8, :] = jnp.broadcast_to(columns[row : row + 8, pick : pick + 1], (8, LANES))


def own_kernel(sources, message, result, here, center, target_rows, radial_side, spread, *, active):
    stars = sources.shape[1]
    spread_columns(sources[...], spread, (0, 1, 2, 4, 5, 6, 7))
    lines = unpack_targets(message[...], active)
    wide = message.shape[0] * active
    blank = jnp.zeros_like(lines[0])
    state = jnp.concatenate(lines[:3] + [blank + 1.0] + lines[3:] + [blank], 0)
    radial_side[...] = target_features(state).astype(BF16)
    middle = 0.5 * (jnp.min(state, 1, keepdims=True) + jnp.max(state, 1, keepdims=True))
    row = row_iota(state.shape)
    middle = jnp.where((row == 3) | (row == 7), 0.0, jnp.broadcast_to(middle, state.shape))
    here[...] = state - middle
    center[...] = middle[:, :LANES]
    for k, line in enumerate(lines[:3]):
        for g in range(wide // LANES):
            target_rows[g, k * 8 : k * 8 + 8, :] = jnp.broadcast_to(line[:, g * LANES : g * LANES + LANES], (8, LANES))
    total = []
    for group in range(wide // LANES):
        own = [jnp.broadcast_to(line[:, group * LANES : group * LANES + LANES], (8, LANES)) for line in lines]

        def one(step, carry):
            sums = list(carry)
            for part in range(4):
                start = pl.multiple_of(step * 32, 32) + part * 8
                there = [spread[k, pl.ds(start, 8), :] for k in range(7)]
                r = [there[k] - own[k] for k in range(3)]
                u = [there[k + 3] - own[k + 3] for k in range(3)]
                q = r[0] * r[0] + r[1] * r[1] + r[2] * r[2] + SOFTENING
                s = r[0] * u[0] + r[1] * u[1] + r[2] * u[2]
                inverse = lax.rsqrt(q)
                squared = inverse * inverse
                weight = there[6] * inverse * squared
                radial = s * squared
                for k in range(3):
                    pull = weight * r[k]
                    sums[k] = sums[k] + pull
                    sums[k + 3] = sums[k + 3] + weight * u[k]
                    sums[k + 6] = sums[k + 6] + radial * pull
            return tuple(sums)

        sums = lax.fori_loop(0, stars // 32, one, (jnp.zeros((8, LANES), F32),) * 9)
        ready = list(sums[:3]) + [sums[k + 3] - 3.0 * sums[k + 6] for k in range(3)]
        total.append([jnp.sum(value, 0, keepdims=True) for value in ready])
    rows = [jnp.concatenate([part[k] for part in total], 1) for k in range(6)]
    result[...] = jnp.concatenate(rows + rows[:2], 0)


def main_kernel(block, sources, own_result, here_rows, center, target_rows, radial_side, result, spread, sum_w, sum_d, *, active):
    blocks, stars = sources.shape[0], sources.shape[2]
    groups = here_rows.shape[1] // LANES
    sum_w[...] = jnp.zeros(sum_w.shape, F32)
    sum_d[...] = jnp.zeros(sum_d.shape, F32)

    def one_block(turn, unused):
        chunk = lax.rem(block[0] + 1 + turn, blocks)
        here = sources[chunk]
        scaled = (here - center[:, :1]) * here[7:8]
        stacked = jnp.concatenate([*three_parts(scaled), jnp.zeros_like(scaled)], 0).astype(BF16)
        radial = source_features(here).T.astype(BF16)
        for step in range(stars // STEP):
            spread_columns(here[:, step * STEP : step * STEP + STEP], spread.at[step], (0, 1, 2))
            part = stacked[:, step * STEP : step * STEP + STEP]
            left = jnp.concatenate([part, part], 1)
            for half in range(groups // 2):
                lanes = slice(half * 2 * LANES, half * 2 * LANES + 2 * LANES)
                some = slice(step * STEP, step * STEP + STEP)
                products = jnp.dot(radial[some], radial_side[:, lanes], preferred_element_type=F32)
                full = [[], [], [], []]
                for row in range(0, STEP, 16):
                    across = [[], [], [], []]
                    for g in (2 * half, 2 * half + 1):
                        own = [target_rows[g, k * 8 : k * 8 + 8, :] for k in range(3)]
                        at_lane = (g - 2 * half) * LANES
                        both_w, both_d = [], []
                        for sub in range(2):
                            top = row + sub * 8
                            there = [spread[step, k, top : top + 8, :] for k in range(3)]
                            r = [there[k] - own[k] for k in range(3)]
                            q = r[0] * r[0] + r[1] * r[1] + (r[2] * r[2] + SOFTENING)
                            s = products[top : top + 8, at_lane : at_lane + LANES]
                            inverse = lax.rsqrt(q)
                            squared = inverse * inverse
                            weight = inverse * squared
                            both_w.append(weight)
                            both_d.append(weight * (s * squared))
                        for at, both in ((0, both_w), (2, both_d)):
                            value = jnp.concatenate(both, 0)
                            upper = value.astype(BF16)
                            across[at].append(upper)
                            across[at + 1].append((value - upper.astype(F32)).astype(BF16))
                    for at in range(4):
                        full[at].append(jnp.concatenate(across[at], 1))
                right_w = jnp.concatenate(full[0] + full[1], 0)
                right_d = jnp.concatenate(full[2] + full[3], 0)
                sum_w[:, lanes] += jnp.dot(left, right_w, preferred_element_type=F32)
                sum_d[:, lanes] += jnp.dot(left, right_d, preferred_element_type=F32)
        return unused

    lax.fori_loop(0, blocks - 1, one_block, 0, unroll=15)
    total_w = sum_w[0:8] + (sum_w[8:16] + sum_w[16:24])
    total_d = sum_d[0:8] + (sum_d[8:16] + sum_d[16:24])
    here = [here_rows[k : k + 1] for k in (0, 1, 2, 4, 5, 6)]
    rows = []
    for k in range(3):
        rows.append(own_result[k : k + 1] + (total_w[k : k + 1] - here[k] * total_w[3:4]))
    for k in range(3):
        straight = total_w[k + 4 : k + 5] - here[k + 3] * total_w[3:4]
        inward = total_d[k : k + 1] - here[k] * total_d[3:4]
        rows.append(own_result[k + 3 : k + 4] + (straight - 3.0 * inward))
    pack_results(rows, active, result)


def final_kernel(parts, accel, jerk, *, active):
    line = jnp.broadcast_to(jnp.sum(parts[...], 0, keepdims=True), (8, LANES))
    for k in range(6):
        turned = pltpu.roll(line, LANES - k * active, 1) if k else line
        (accel if k < 3 else jerk)[k % 3 : k % 3 + 1, :] = turned[k : k + 1, :active]


def keep_near(value):
    return pltpu.with_memory_space_constraint(value, pltpu.VMEM)


def near(*lengths):
    return pltpu.VMEM(lengths, F32)


def shape(*lengths):
    return jax.ShapeDtypeStruct(lengths, F32)


def local(position, velocity, accel_old, jerk_old, mass, elapsed, active_index):
    stars, active = position.shape[1], active_index.shape[0]
    blocks, members = lax.axis_size("blk"), lax.axis_size("grp")
    block = lax.axis_index("blk")
    first = ((block * members + lax.axis_index("grp")) * stars)[None]
    scalar = pl.BlockSpec(memory_space=pltpu.SMEM)
    vector = pl.BlockSpec(memory_space=pltpu.VMEM)
    predicted, sources, targets, mine = pl.pallas_call(
        prologue_kernel,
        out_shape=(shape(6, stars), shape(blocks, 8, stars), near(members, LANES), near(8, stars)),
        in_specs=[scalar] + [vector] * 7,
        name="prologue",
    )(first, active_index[None], position, velocity, accel_old, jerk_old, mass[None], elapsed[None])
    message = lax.all_to_all(targets, "grp", 0, 0, tiled=True)
    gathered = lax.all_to_all(sources, "blk", 0, 0, tiled=True)
    result = interact(block[None], mine, gathered, message, active)
    parts = lax.all_to_all(result, "grp", 0, 0, tiled=True)
    parts = keep_near(parts)
    accel, jerk = pl.pallas_call(
        lambda *refs: final_kernel(*refs, active=active), out_shape=(shape(3, active), shape(3, active)), name="final"
    )(parts)
    return (predicted, accel, jerk)


def interact(block, mine, gathered, message, active):
    stars, wide = mine.shape[1], message.shape[0] * active
    groups = wide // LANES
    scalar = pl.BlockSpec(memory_space=pltpu.SMEM)
    vector = pl.BlockSpec(memory_space=pltpu.VMEM)
    mine, message = keep_near(mine), keep_near(message)
    prepared = pl.pallas_call(
        lambda *refs: own_kernel(*refs, active=active),
        out_shape=(near(8, wide), near(8, wide), near(8, LANES), near(groups, 24, LANES), pltpu.VMEM((LANES, wide), BF16)),
        scratch_shapes=[pltpu.VMEM((7, stars, LANES), F32)],
        name="own",
    )(mine, message)
    return pl.pallas_call(
        lambda *refs: main_kernel(*refs, active=active),
        out_shape=near(message.shape[0], LANES),
        in_specs=[scalar] + [vector] * 6,
        scratch_shapes=[
            pltpu.VMEM((stars // STEP, 3, STEP, LANES), F32),
            pltpu.VMEM((32, wide), F32),
            pltpu.VMEM((32, wide), F32),
        ],
        name="interact",
    )(block, keep_near(gathered), *[keep_near(value) for value in prepared])


def solution(mesh):
    whole = P(None, ("blk", "grp"))
    flat = P(("blk", "grp"))
    return jax.shard_map(
        local,
        mesh=mesh,
        in_specs=(whole, whole, whole, whole, flat, flat, flat),
        out_specs=(whole, whole, whole),
        check_vma=False,
    )
```
